256 devices in a mesh: row: 8 (over y_lo, x), col: 16 (over z, core), rep: 2 (over y_hi).
Axes of the slice: x: 4, y: 4 (y_hi: 2, y_lo: 2; y = y_hi * 2 + y_lo), z: 8, core: 2. Of those that a mesh axis runs over, the one named last changes fastest.
Arguments:
- diag_parts: float32 [2, 2, 512, 512], P('rep', None, 'row', 'col'), may hold values from -6 to 6
- row_parts: float32 [2, 2, 512, 8192], P('rep', None, 'row', 'col'), may hold values from -6 to 6
- col_parts: float32 [2, 2, 8192, 512], P('rep', None, 'row', 'col'), may hold values from -6 to 6
- trail_parts: float32 [2, 2, 8192, 8192], P('rep', None, 'row', 'col'), may hold values from -6 to 6
- pivot_rows: int32 [512], replicated, may hold values from 0 to 8191, as said below
- lower_inverse: float32 [2, 512, 512], P(None, 'rep'), may hold values from -1 to 1, as said below
- upper_inverse: float32 [2, 512, 512], P(None, None, 'rep'), may hold values from -1 to 1, as said below
Outputs:
- lower_factor: float32 [2, 8192, 512], P(None, 'row', 'rep')
- upper_factor: float32 [2, 512, 8192], P(None, 'rep', 'col')
- trailing_out: float32 [2, 2, 8192, 8192], P('rep', None, 'row', 'col')
The draws below stay inside these ranges and needn't reach their ends.
Inputs may be any that keep to these rules, and one draw needn't show every extreme that they name: `pivot_rows`: 512 distinct rows of the trailing block; 0 and 8191 are always among them. `lower_inverse`: unit lower triangular in the real part, strictly lower triangular in the imaginary part. `upper_inverse`: upper triangular in both parts.
All inputs are finite; a program needn't handle non-finite values.
Results may differ from the reference program's by a relative error of at most 0.0001.
Values sent between devices are 32-bit elements; how exact they have to be, the bound alone decides.
No kernel may reach another device: no remote copies, remote signals or barrier semaphores. Data moves between devices by JAX's collectives and lax.ppermute only.
A program may use at most 128 MiB of HBM per device.

```python
import jax
import jax.numpy as jnp
from jax import lax

NB = 512
M = 8192
REP = 2
KH = 256


def draw_pivot_rows(key, part):
    picked = jax.random.permutation(key, M)[:NB].astype(jnp.int32)
    lowest = jnp.min(picked)
    highest = jnp.max(picked)
    picked = jnp.where(picked == lowest, 0, picked)
    picked = jnp.where(picked == highest, M - 1, picked)
    return picked.astype(jnp.int32)


def draw_lower_inverse(key, part):
    first_key, second_key = jax.random.split(jax.random.fold_in(key, 11))
    rows_grid = jnp.arange(NB)[:, None]
    cols_grid = jnp.arange(NB)[None, :]
    strict = (rows_grid > cols_grid).astype(jnp.float32)
    spread = (3.0 / NB) ** 0.5
    real_part = jnp.eye(NB, dtype=jnp.float32) + strict * jax.random.uniform(first_key, (NB, NB), jnp.float32, -spread, spread)
    imag_part = strict * jax.random.uniform(second_key, (NB, NB), jnp.float32, -spread, spread)
    return jnp.stack([real_part, imag_part])


def draw_upper_inverse(key, part):
    first_key, second_key = jax.random.split(jax.random.fold_in(key, 23))
    rows_grid = jnp.arange(NB)[:, None]
    cols_grid = jnp.arange(NB)[None, :]
    upper_mask = (rows_grid <= cols_grid).astype(jnp.float32)
    spread = 0.05 * (3.0 / NB) ** 0.5
    real_part = upper_mask * jax.random.uniform(first_key, (NB, NB), jnp.float32, -spread, spread)
    imag_part = upper_mask * jax.random.uniform(second_key, (NB, NB), jnp.float32, -spread, spread)
    return jnp.stack([real_part, imag_part])


def levels(rng, dims, cuts, low, largest):
    loudness, own = 1.0, jax.random.fold_in(rng, 6)
    for position, parts in cuts:
        draws = jnp.exp(jax.random.uniform(jax.random.fold_in(own, position), (parts,), jnp.float32, low / len(cuts), largest / len(cuts)))
        loudness = loudness * jnp.repeat(draws, dims[position] // parts).reshape([-1 if axis == position else 1 for axis in range(len(dims))])
    return loudness


def scatter_about(own_key, shape, scale, bound, cuts=(), held_as=jnp.bfloat16):
    level = levels(own_key, shape, cuts, -0.22, 0.18) if cuts else 1.0
    entries = jax.random.normal(own_key, shape, jnp.float32) * scale * level
    return jnp.minimum(jnp.maximum(entries, -bound), bound).astype(held_as)


def setup_inputs(seed: int = 0) -> dict:
    seeds = jax.random.split(jax.random.key(seed), 8)
    return {
        "diag_parts": scatter_about(seeds[0], (REP, 2, NB, NB), 1.0, 6.0, ((0, 2), (2, 8), (3, 16)), jnp.float32),
        "row_parts": scatter_about(seeds[1], (REP, 2, NB, M), 1.0, 6.0, ((0, 2), (2, 8), (3, 16)), jnp.float32),
        "col_parts": scatter_about(seeds[2], (REP, 2, M, NB), 1.0, 6.0, ((0, 2), (2, 8), (3, 16)), jnp.float32),
        "trail_parts": scatter_about(seeds[3], (REP, 2, M, M), 1.0, 6.0, ((0, 2), (2, 8), (3, 16)), jnp.float32),
        "pivot_rows": draw_pivot_rows(jax.random.fold_in(seeds[7], 71), 0),
        "lower_inverse": draw_lower_inverse(jax.random.fold_in(seeds[7], 71), 0),
        "upper_inverse": draw_upper_inverse(jax.random.fold_in(seeds[7], 71), 0),
    }


def complex_dot(left_real, left_imag, right_real, right_imag):
    high = lax.Precision.HIGHEST
    real_part = jnp.dot(left_real, right_real, precision=high, preferred_element_type=jnp.float32) - jnp.dot(left_imag, right_imag, precision=high, preferred_element_type=jnp.float32)
    imag_part = jnp.dot(left_real, right_imag, precision=high, preferred_element_type=jnp.float32) + jnp.dot(left_imag, right_real, precision=high, preferred_element_type=jnp.float32)
    return real_part, imag_part


def reference(diag_parts, row_parts, col_parts, trail_parts, pivot_rows, lower_inverse, upper_inverse):
    pivots = pivot_rows.astype(jnp.int32)
    swapped_col = col_parts.at[:, :, pivots, :].set(diag_parts)
    panel_col = jnp.sum(swapped_col, axis=0)
    panel_row = jnp.sum(trail_parts[:, :, pivots, :], axis=0)
    swapped_trail = trail_parts.at[:, :, pivots, :].set(row_parts)
    lower_real, lower_imag = complex_dot(panel_col[0], panel_col[1], upper_inverse[0], upper_inverse[1])
    upper_real, upper_imag = complex_dot(lower_inverse[0], lower_inverse[1], panel_row[0], panel_row[1])
    layers_out = []
    for layer_index in range(REP):
        begin = layer_index * KH
        update_real, update_imag = complex_dot(lower_real[:, begin:begin + KH], lower_imag[:, begin:begin + KH], upper_real[begin:begin + KH], upper_imag[begin:begin + KH])
        layers_out.append(jnp.stack([swapped_trail[layer_index, 0] - update_real, swapped_trail[layer_index, 1] - update_imag]))
    lower_factor = jnp.stack([lower_real, lower_imag])
    upper_factor = jnp.stack([upper_real, upper_imag])
    return lower_factor, upper_factor, jnp.stack(layers_out)
```

```python
import jax
import jax.numpy as jnp
from jax import lax
from jax.experimental import pallas as pl
from jax.experimental.pallas import tpu as pltpu
from jax.sharding import PartitionSpec as P

CAP_P = 56
CAP_R = 24
LOAD = CAP_P + 32
ROWS = 512
ALL = ("row", "col", "rep")


def place(x, y, z, c):
    row = (y % 2) * 4 + x
    return (row * 16 + z * 2 + c) * 2 + y // 2


def permutation(move):
    pairs = []
    for x in range(4):
        for y in range(4):
            for z in range(8):
                for c in range(2):
                    pairs.append((place(x, y, z, c), place(*move(x, y, z, c))))
    return pairs


def plane_step(stage, sign):
    def move(x, y, z, c):
        if (c == 0) == (stage == 0):
            return ((x + sign) % 4, y, z, c)
        return (x, (y + sign) % 4, z, c)

    return permutation(move)


Z_STEP = permutation(lambda x, y, z, c: (x, y, (z + (1 if c == 0 else -1)) % 8, c))
CORE_SWAP = permutation(lambda x, y, z, c: (x, y, z, 1 - c))
REP_SWAP = [(0, 1), (1, 0)]


def split(v):
    hi = v.astype(jnp.bfloat16)
    return hi, (v - hi.astype(jnp.float32)).astype(jnp.bfloat16)


def pieces(v):
    hi = v.astype(jnp.bfloat16)
    return (hi, *split(v - hi.astype(jnp.float32)))


def mxu(a, b):
    return jnp.dot(a, b, preferred_element_type=jnp.float32)


def as_column(line):
    return jnp.broadcast_to(line.astype(jnp.float32), (128, line.shape[1])).T


def marks(column, width, offset=0):
    lane = lax.broadcasted_iota(jnp.int32, column.shape, 1).astype(jnp.float32)
    blocks = [(column == lane + float(offset + 128 * k)) for k in range(-(-width // 128))]
    return jnp.concatenate(blocks, axis=1)[:, :width].astype(jnp.float32).astype(jnp.bfloat16)


def gather_kernel(rows_ref, trail_ref, diag_ref, out_ref):
    both = jnp.concatenate([diag_ref[0], diag_ref[1]], axis=1)
    for part in range(2):
        for block in range(4):
            for half in range(2):
                out_ref[part, block, half, CAP_P:LOAD, :] = both
    for half in range(2):

        def step(s, carry, half=half):
            at = rows_ref[half * CAP_P + s]
            for part in range(2):
                line = trail_ref[part, pl.ds(at, 1), :]
                for block in range(4):
                    out_ref[part, block, half, pl.ds(s, 1), :] = line[:, block * 128 : (block + 1) * 128]
            return carry

        lax.fori_loop(0, CAP_P, step, 0, unroll=8)


def dense_kernel(from_ref, got_ref, out_ref):
    total = (got_ref[:, 0, :CAP_P] + got_ref[:, 1, :CAP_P]).reshape(8 * CAP_P, 128)
    right = jnp.concatenate(pieces(total), axis=1)
    res = mxu(marks(as_column(from_ref[...]), 8 * CAP_P), right)
    out_ref[...] = (res[:, 0:128] + res[:, 128:256]) + res[:, 256:384]


def pack_rows(key_ref, rows_ref, out_ref):
    slot = lax.broadcasted_iota(jnp.int32, (8 * CAP_R, 64), 0)
    pick = (slot == key_ref[...]).astype(jnp.float32).astype(jnp.bfloat16)
    for part in range(2):
        hi, mid, lo = pieces(rows_ref[part])
        res = (mxu(pick, hi) + mxu(pick, mid)) + mxu(pick, lo)
        for dst in range(8):
            out_ref[dst, part] = res[dst * CAP_R : (dst + 1) * CAP_R]


def find_landing(spot_ref, slot_ref, lands_ref):
    spot, slot = as_column(spot_ref[...]), as_column(slot_ref[...])
    lane = lax.broadcasted_iota(jnp.int32, spot.shape, 1).astype(jnp.float32)
    for block in range(8):
        hit = jnp.where(spot == lane + float(128 * block), slot, -1.0)
        lands_ref[:, block * 128 : (block + 1) * 128] = jnp.max(hit, axis=0, keepdims=True).astype(jnp.int32)


def spill_prep_kernel(key_ref, rows_ref, spot_ref, slot_ref, out_ref, lands_ref):
    pack_rows(key_ref, rows_ref, out_ref)
    find_landing(spot_ref, slot_ref, lands_ref)


def prep_kernel(
    place_ref, key_ref, rows_ref, spot_ref, slot_ref, inv_ref, out_ref, lands_ref, left_ref,
):
    pack_rows(key_ref, rows_ref, out_ref)
    find_landing(spot_ref, slot_ref, lands_ref)
    a, b = inv_ref[0].T, inv_ref[1].T
    for n, v in enumerate((a, b - a, a + b)):
        hi, lo = split(v)
        left_ref[n] = jnp.concatenate([hi, hi, lo], axis=1)


def column_kernel(spot_ref, own_ref, other_ref, diag_ref, out_ref):
    low = lax.broadcasted_iota(jnp.int32, (32, 128), 1) < 64
    reals, imags = [], []
    for src in range(0, 8, 2):
        even = diag_ref[2 * src, CAP_P:] + diag_ref[2 * src + 1, CAP_P:]
        odd = diag_ref[2 * src + 2, CAP_P:] + diag_ref[2 * src + 3, CAP_P:]
        reals.append(jnp.where(low, even, pltpu.roll(odd, 64, 1)))
        imags.append(jnp.where(low, pltpu.roll(even, 64, 1), odd))
    left = jnp.concatenate([jnp.concatenate(reals, axis=1), jnp.concatenate(imags, axis=1)], axis=0)
    stack = jnp.concatenate([*pieces(left), jnp.ones((32, 512), jnp.bfloat16)], axis=0)
    column = as_column(spot_ref[...])
    for part in range(4):
        cols = slice(part * 256, (part + 1) * 256)
        res = mxu(stack, marks(column, 256, part * 256))
        moved = (res[0:64] + res[64:128]) + res[128:192]
        stay = res[192:224] < 0.5
        for ri in range(2):
            kept = own_ref[ri, :, cols] + other_ref[ri, :, cols]
            out_ref[ri, :, cols] = jnp.where(stay, kept, moved[ri * 32 : (ri + 1) * 32])


def start_all(pairs, sems):
    copies = [pltpu.make_async_copy(src, dst, sems.at[n]) for n, (src, dst) in enumerate(pairs)]
    for copy in copies:
        copy.start()
    return copies


def wait_all(copies):
    for copy in copies:
        copy.wait()


def lower_kernel(place_ref, *refs):
    q, t1, t2, t3, t4, w1, w2, w3, w4, left = refs[:10]
    low_ref, low3_ref, col, low, sem, in_sem = refs[10:]
    z, c = place_ref[2], place_ref[3]
    step = 2 * c - 1
    moves = []

    def put(ref, at, core):
        moves.append((ref, col.at[at, core]))

    put(q.at[0], z, c)
    put(q.at[1], z, 1 - c)
    for k, t, w in ((1, t1, w1), (2, t2, w2), (3, t3, w3)):
        put(t.at[0], (z + k * step) & 7, c)
        put(t.at[1], (z + k * step) & 7, 1 - c)
        put(w.at[0], (z - k * step) & 7, 1 - c)
        put(w.at[1], (z - k * step) & 7, c)
    put(t4, (z + 4) & 7, c)
    put(w4, (z + 4) & 7, 1 - c)
    wait_all(start_all(moves, in_sem))
    copies = []
    for block in range(1024 // ROWS):
        rows = slice(block * ROWS, (block + 1) * ROWS)
        re = col[:, :, 0, :, rows].reshape(512, ROWS)
        im = col[:, :, 1, :, rows].reshape(512, ROWS)
        k = []
        for n, v in enumerate((re + im, re, im)):
            hi, lo = split(v)
            k.append(mxu(left[n], jnp.concatenate([hi, lo, hi], axis=0)))
        lr, li = (k[0] - k[2]).T, (k[0] + k[1]).T
        low[0, rows] = lr
        low[1, rows] = li
        for n, v in enumerate((lr + li, lr, li)):
            hi, lo = split(v)
            low3_ref[n, rows] = jnp.concatenate([hi, lo, hi], axis=1)
        for part in range(2):
            copy = pltpu.make_async_copy(low.at[part, rows], low_ref.at[part, rows], sem.at[2 * block + part])
            copy.start()
            copies.append(copy)
    for copy in copies:
        copy.wait()


def upper_kernel(
    place_ref, b0, s_prev, s_next, far_a, far_b, inv_ref, got_ref, up_ref, right_ref, moved_ref, mats, up, up_sem, in_sem,
):
    x, y, c = place_ref[0], place_ref[1], place_ref[3]
    stacks = ((b0, (0, 1, 2, 3), 0), (s_next, (0, 1, 2, 3), 1), (s_prev, (0, 1, 2, 3), 3), (far_a, (0, 1), 2), (far_b, (2, 3), 2))
    moves = []
    for ref, firsts, second in stacks:
        for at, first in enumerate(firsts):
            dx = jnp.where(c == 0, first, second)
            dy = jnp.where(c == 0, second, first)
            xx, yy = (x + dx) & 3, (y + dy) & 3
            moves.append((ref.at[at], mats.at[yy & 1, yy >> 1, xx]))
    copies = start_all(moves, in_sem)
    a, b = inv_ref[0], inv_ref[1]
    left_ref = []
    for v in (a + b, a, b):
        hi, lo = split(v)
        left_ref.append(jnp.concatenate([hi, hi, lo], axis=1))
    for part in range(2):
        rows = jnp.concatenate([got_ref[src, part] for src in range(8)], axis=0)
        moved_ref[part] = jnp.concatenate(pieces(rows), axis=0)
    wait_all(copies)
    for pair in range(2):
        cols = slice(pair * 256, (pair + 1) * 256)

        def take(part):
            tops = jnp.concatenate([mats[part, 0, 2 * pair], mats[part, 0, 2 * pair + 1]], axis=1)
            lows = jnp.concatenate([mats[part, 1, 2 * pair], mats[part, 1, 2 * pair + 1]], axis=1)
            return jnp.concatenate([tops, lows], axis=0)

        re, im = take(0), take(1)
        k = []
        for n, v in enumerate((re, im - re, re + im)):
            hi, lo = split(v)
            k.append(mxu(left_ref[n], jnp.concatenate([hi, lo, hi], axis=0)))
        a, b = k[0] - k[2], k[0] + k[1]
        up[0, :, cols] = a
        up[1, :, cols] = b
        for n, v in enumerate((a, b - a, a + b)):
            hi, lo = split(v)
            right_ref[n, :, cols] = jnp.concatenate([hi, hi, lo], axis=0)
    copy = pltpu.make_async_copy(up, up_ref, up_sem)
    copy.start()
    copy.wait()


def tail_kernel(right, low3_ref, trail_ref, lands_ref, moved, out_ref, out, trail, sem, in_sem):
    half = 1024 // 2
    arriving = start_all(
        [(trail_ref.at[:, pl.ds(n * half, half)], trail.at[:, pl.ds(n * half, half)]) for n in range(2)], in_sem
    )
    copies = []
    for block in range(1024 // ROWS):
        rows = slice(block * ROWS, (block + 1) * ROWS)
        column = as_column(lands_ref[:, rows])
        pick = marks(column, 8 * CAP_R)
        pick = jnp.concatenate([pick, pick, pick], axis=1)
        stays = jnp.concatenate([column] * 4, axis=1) < 0.0
        k = [mxu(low3_ref[n, rows], right[n]) for n in range(3)]
        arriving[block].wait()
        for part, update in enumerate((k[0] - k[2], k[0] + k[1])):
            base = jnp.where(stays, trail[part, rows], 0.0) + mxu(pick, moved[part])
            out[part, rows] = base - update
            copy = pltpu.make_async_copy(out.at[part, rows], out_ref.at[0, part, rows], sem.at[2 * block + part])
            copy.start()
            copies.append(copy)
    for copy in copies:
        copy.wait()


def spill_kernel(lands_ref, got_ref, old_ref, out_ref):
    pick = marks(as_column(lands_ref[...]), 8 * CAP_R)
    for part in range(2):
        rows = jnp.concatenate([got_ref[src, part] for src in range(8)], axis=0)
        hi, mid, lo = pieces(rows)
        out_ref[0, part] = old_ref[0, part] + ((mxu(pick, hi) + mxu(pick, mid)) + mxu(pick, lo))


def step(diag_parts, row_parts, col_parts, trail_parts, pivot_rows, lower_inverse, upper_inverse):
    row = lax.axis_index("row")
    column = lax.axis_index("col")
    rep = lax.axis_index("rep")
    c = column & 1
    where_am_i = jnp.stack([row & 3, rep * 2 + (row >> 2), column >> 1, c]).astype(jnp.int32)
    trail = trail_parts[0]
    rowp = row_parts[0]
    col_t = jnp.swapaxes(col_parts[0], 1, 2)
    diag_t = jnp.swapaxes(diag_parts[0], 1, 2)
    smem = pl.BlockSpec(memory_space=pltpu.SMEM)
    vmem = pl.BlockSpec(memory_space=pltpu.VMEM)

    def f32(*shape):
        return jax.ShapeDtypeStruct(shape, jnp.float32)

    def whole(kernel, out, *args, small=0, scratch=()):
        specs = [smem] * small + [vmem] * (len(args) - small)
        return pl.pallas_call(
            kernel, out_shape=out, in_specs=specs, out_specs=jax.tree.map(lambda _: vmem, out),
            scratch_shapes=list(scratch),
            compiler_params=pltpu.CompilerParams(vmem_limit_bytes=20 * 2**20),
        )(*args)

    def send(value, pairs, axes=ALL):
        return lax.ppermute(value, axes, pairs)

    def exchange(value, axes):
        return lax.all_to_all(value, axes, 0, 0, tiled=True)

    other_col = send(col_t, REP_SWAP, "rep")
    owner, spot = pivot_rows >> 10, pivot_rows & 1023
    order = jnp.arange(512, dtype=jnp.int32)
    before = (owner[:, None] == owner[None, :]) & (order[:, None] < order[None, :])
    same_half = (order[:, None] >> 8) == (order[None, :] >> 8)
    same_src = (order[:, None] >> 6) == (order[None, :] >> 6)
    rank_p = jnp.sum((before & same_half).astype(jnp.int32), axis=0)
    mine = owner == row

    def packed_panel(turn):
        at = rank_p - turn * CAP_P
        slot = jnp.where(mine & (at >= 0) & (at < CAP_P), (order >> 8) * CAP_P + at, -1)
        wanted = jnp.arange(2 * CAP_P, dtype=jnp.int32)[:, None] == slot[None, :]
        source = jnp.max(jnp.where(wanted, spot[None, :], 0), axis=1)
        return whole(gather_kernel, f32(2, 4, 2, LOAD, 128), source, trail, diag_t, small=1)

    def dense(turn, got):
        at = rank_p - turn * CAP_P
        place_at = jnp.where((at >= 0) & (at < CAP_P), owner * CAP_P + at, -1)
        here = lax.dynamic_slice_in_dim(place_at, rep * 256, 256)[None]
        return whole(dense_kernel, f32(256, 128), here, got.reshape(8, 2, LOAD, 128))

    packed = packed_panel(0)
    arrived = exchange(packed.reshape(16, LOAD, 128), ("row", "rep"))

    spots = jnp.where(mine, spot, -1)[None]
    most_p = jnp.max(rank_p)
    rank_r = jnp.sum((before & same_src).astype(jnp.int32), axis=0)
    most_r = jnp.max(rank_r)

    def swap_lists(turn, overflow):
        at = rank_r - turn * CAP_R
        fits = (at >= 0) & (at < CAP_R)
        key = jnp.where(fits, owner * CAP_R + at, -1)
        here = lax.dynamic_slice_in_dim(key, row * 64, 64)[None]
        slot = jnp.where(fits, (order >> 6) * CAP_R + at, overflow)
        return here, rowp, spots, slot[None]

    lands_shape = jax.ShapeDtypeStruct((1, 1024), jnp.int32)
    thirds = jax.ShapeDtypeStruct((3, 256, 1536), jnp.bfloat16)
    row_packed, lands, left = whole(
        prep_kernel, (f32(8, 2, CAP_R, 512), lands_shape, thirds),
        where_am_i, *swap_lists(0, 1023), upper_inverse, small=1,
    )

    col_sum = whole(column_kernel, f32(2, 32, 1024), spots, col_t, other_col, arrived)
    panel = dense(0, arrived)

    def more_panel(state):
        got = exchange(packed_panel(state[0]).reshape(16, LOAD, 128), ("row", "rep"))
        return state[0] + 1, state[1] + dense(state[0], got)

    panel = lax.while_loop(lambda s: s[0] * CAP_P <= most_p, more_panel, (jnp.int32(1), panel))[1]

    chip = jnp.stack([col_sum, send(col_sum, CORE_SWAP)])
    t1 = send(chip, Z_STEP)
    t2 = send(t1, Z_STEP)
    w1 = send(t1, CORE_SWAP)
    t3 = send(t2, Z_STEP)
    w2 = send(t2, CORE_SWAP)
    t4 = send(t3[0], Z_STEP)
    w3 = send(t3, CORE_SWAP)
    w4 = send(t4, CORE_SWAP)

    r_prev = send(panel, plane_step(0, 1))
    r_next = send(panel, plane_step(0, -1))
    r_far = send(panel, plane_step(0, 2))
    b0 = jnp.stack([panel, r_next, r_far, r_prev])
    s_prev = send(b0, plane_step(1, 1))
    s_next = send(b0, plane_step(1, -1))
    s_far_a = send(s_prev[:2], plane_step(1, 1))
    s_far_b = send(s_next[2:], plane_step(1, -1))
    got = exchange(row_packed, "row")

    rows = 256
    hbm = pl.BlockSpec(memory_space=pl.ANY)
    blocks = 1024 // ROWS
    sems = pltpu.SemaphoreType.DMA((2 * blocks,))

    def call(kernel, mb, out, out_specs, scratch, in_specs, *args):
        return pl.pallas_call(
            kernel,
            out_shape=out,
            in_specs=in_specs,
            out_specs=out_specs,
            scratch_shapes=scratch,
            compiler_params=pltpu.CompilerParams(vmem_limit_bytes=mb * 2**20),
        )(*args)

    def bf16(*shape):
        return jax.ShapeDtypeStruct(shape, jnp.bfloat16)

    upper, right, moved = call(
        upper_kernel, 20, (f32(2, 256, 512), bf16(3, 768, 512), bf16(2, 24 * CAP_R, 512)), (hbm, vmem, vmem),
        [
            pltpu.VMEM((2, 2, 4, 256, 128), jnp.float32),
            pltpu.VMEM((2, 256, 512), jnp.float32),
            pltpu.SemaphoreType.DMA,
            pltpu.SemaphoreType.DMA((16,)),
        ],
        [smem] + [hbm] * 5 + [vmem] * 2, where_am_i, b0, s_prev, s_next, s_far_a, s_far_b, lower_inverse, got,
    )
    lower, low3 = call(
        lower_kernel, 28, (f32(2, 1024, 256), bf16(3, 1024, 768)), (hbm, vmem),
        [
            pltpu.VMEM((8, 2, 2, 32, 1024), jnp.float32),
            pltpu.VMEM((2, 1024, 256), jnp.float32),
            sems,
            pltpu.SemaphoreType.DMA((16,)),
        ],
        [smem] + [hbm] * 9 + [vmem], where_am_i, chip, t1, t2, t3, t4, w1, w2, w3, w4, left,
    )
    trailing = call(
        tail_kernel, 28, f32(1, 2, 1024, 512), hbm,
        [
            pltpu.VMEM((2, 1024, 512), jnp.float32),
            pltpu.VMEM((2, 1024, 512), jnp.float32),
            sems,
            pltpu.SemaphoreType.DMA((2,)),
        ],
        [vmem, vmem, hbm, vmem, vmem], right, low3, trail, lands, moved,
    )

    def more_rows(state):
        turn, old = state
        send_rows, late = whole(spill_prep_kernel, (f32(8, 2, CAP_R, 512), lands_shape), *swap_lists(turn, -1))
        block = pl.BlockSpec((1, 2, rows, 512), lambda i: (0, 0, i, 0))
        new = pl.pallas_call(
            spill_kernel,
            out_shape=f32(1, 2, 1024, 512),
            grid=(1024 // rows,),
            in_specs=[
                pl.BlockSpec((1, rows), lambda i: (0, i)),
                pl.BlockSpec((8, 2, CAP_R, 512), lambda i: (0, 0, 0, 0)),
                block,
            ],
            out_specs=block,
            input_output_aliases={2: 0},
            name="spill",
        )(late, exchange(send_rows, "row"), old)
        return turn + 1, new

    trailing = lax.while_loop(lambda s: s[0] * CAP_R <= most_r, more_rows, (jnp.int32(1), trailing))[1]
    return lower, upper, trailing


def solution(mesh):
    in_specs = (
        P("rep", None, "row", "col"),
        P("rep", None, "row", "col"),
        P("rep", None, "row", "col"),
        P("rep", None, "row", "col"),
        P(),
        P(None, "rep", None),
        P(None, None, "rep"),
    )
    out_specs = (P(None, "row", "rep"), P(None, "rep", "col"), P("rep", None, "row", "col"))
    return jax.shard_map(step, mesh=mesh, in_specs=in_specs, out_specs=out_specs, check_vma=False)
```
